32 devices in a mesh: dp: 8 (over z, y), sub: 4 (over x, core).
Axes of the slice: x: 2, y: 2, z: 4, core: 2. Of those that a mesh axis runs over, the one named last changes fastest.
Arguments:
- inputs: bfloat16 [2, 32, 512, 1024], P(None, ('dp', 'sub')), may hold values from -6 to 6
- cotangent: bfloat16 [2, 32, 512, 1024], P(None, ('dp', 'sub')), may hold values from -6 to 6
- lengths: int32 [2, 32, 4], P(None, ('dp', 'sub')), may hold values from 1 to 256, 512 in all within a row
- weight_qkv: float32 [1024, 3072], P(('dp', 'sub')), may hold values from -0.1875 to 0.1875
- weight_out: float32 [1024, 1024], P(('dp', 'sub')), may hold values from -0.1875 to 0.1875
- weight_up: float32 [1024, 4096], P(('dp', 'sub')), may hold values from -0.1875 to 0.1875
- weight_down: float32 [4096, 1024], P(('dp', 'sub')), may hold values from -0.09375 to 0.09375
- param_table: float32 [22, 1024], P(None, ('dp', 'sub')), may hold values from -0.8 to 1.6
- head_scale: float32 [16], replicated, may hold values from 0.5 to 2
- moment_qkv: float32 [1024, 3072], P(('dp', 'sub')), may hold values from -1024 to 1024
- square_qkv: float32 [1024, 3072], P(('dp', 'sub')), may hold values from 16384 to 262144
- moment_out: float32 [1024, 1024], P(('dp', 'sub')), may hold values from -1024 to 1024
- square_out: float32 [1024, 1024], P(('dp', 'sub')), may hold values from 16384 to 262144
- moment_up: float32 [1024, 4096], P(('dp', 'sub')), may hold values from -1024 to 1024
- square_up: float32 [1024, 4096], P(('dp', 'sub')), may hold values from 16384 to 262144
- moment_down: float32 [4096, 1024], P(('dp', 'sub')), may hold values from -1024 to 1024
- square_down: float32 [4096, 1024], P(('dp', 'sub')), may hold values from 16384 to 262144
- moment_table: float32 [22, 1024], P(None, ('dp', 'sub')), may hold values from -1024 to 1024
- square_table: float32 [22, 1024], P(None, ('dp', 'sub')), may hold values from 16384 to 262144
- moment_heads: float32 [16], replicated, may hold values from -1024 to 1024
- square_heads: float32 [16], replicated, may hold values from 16384 to 262144
Outputs:
- layer_out: bfloat16 [2, 32, 512, 1024], P(None, ('dp', 'sub'))
- input_grad: float32 [2, 32, 512, 1024], P(None, ('dp', 'sub'))
- new_weight_qkv: float32 [1024, 3072], P(('dp', 'sub'))
- new_moment_qkv: float32 [1024, 3072], P(('dp', 'sub'))
- new_square_qkv: float32 [1024, 3072], P(('dp', 'sub'))
- new_weight_out: float32 [1024, 1024], P(('dp', 'sub'))
- new_moment_out: float32 [1024, 1024], P(('dp', 'sub'))
- new_square_out: float32 [1024, 1024], P(('dp', 'sub'))
- new_weight_up: float32 [1024, 4096], P(('dp', 'sub'))
- new_moment_up: float32 [1024, 4096], P(('dp', 'sub'))
- new_square_up: float32 [1024, 4096], P(('dp', 'sub'))
- new_weight_down: float32 [4096, 1024], P(('dp', 'sub'))
- new_moment_down: float32 [4096, 1024], P(('dp', 'sub'))
- new_square_down: float32 [4096, 1024], P(('dp', 'sub'))
- new_table: float32 [22, 1024], P(None, ('dp', 'sub'))
- new_moment_table: float32 [22, 1024], P(None, ('dp', 'sub'))
- new_square_table: float32 [22, 1024], P(None, ('dp', 'sub'))
- new_heads: float32 [16], replicated
- new_moment_heads: float32 [16], replicated
- new_square_heads: float32 [16], replicated
- lamb_stats: float32 [4, 3], replicated
The draws below stay inside these ranges and needn't reach their ends.
Inputs may be any that keep to these rules, and one draw needn't show every extreme that they name: In every row the 4 lengths sum to 512 and the longest is 256; the last of them is the row's padding tail.
All inputs are finite; a program needn't handle non-finite values.
Results may differ from the reference program's by a relative error of at most 0.012.
Values may be sent and summed in bfloat16 or wider, within the bound.
No kernel may reach another device: no remote copies, remote signals or barrier semaphores. Data moves between devices by JAX's collectives and lax.ppermute only.
A program may use at most 256 MiB of HBM per device.

```python
import math
import jax
import jax.numpy as jnp
import numpy as np
from jax import lax

D = 1024
HEADS = 16
HD = 64
FF = 4096
SEQ = 512
MB = 2
NDOC = 4
STEP = 5
BATCH = 32
TOKENS = 32768
VR = 22


def draw_param_table(key, part):
    blocks = FF // D
    count = 10 + 3 * blocks
    noise = jnp.clip(jax.random.normal(key, (count, D), jnp.float32), -4.0, 4.0)
    row_ids = jnp.arange(count)[:, None]
    return jnp.where(row_ids < 3 + blocks, 1.0 + 0.15 * noise, 0.2 * noise)


def steps_of(rng, shape, split, least, top_value):
    level, own = 1.0, jax.random.fold_in(rng, 6)
    for axis_at, blocks in split:
        draws = jnp.exp(jax.random.uniform(jax.random.fold_in(own, axis_at), (blocks,), jnp.float32, least / len(split), top_value / len(split)))
        level = level * jnp.repeat(draws, shape[axis_at] // blocks).reshape([-1 if axis == axis_at else 1 for axis in range(len(shape))])
    return level


def length_profile(count, total, limit, slope):
    loads = [(1 << 20) // math.isqrt(standing ** slope) + 1 for standing in range(2, count + 1)]
    rest, counts = total - limit - (count - 1), [1] * (count - 1)
    while rest > 0:
        free = [i for i in range(count - 1) if counts[i] < limit]
        pool, left = sum([loads[i] for i in free]), rest
        for i in free:
            more = min(limit - counts[i], max(1, left * loads[i] // pool), rest)
            counts[i] = counts[i] + more
            rest = rest - more
    return np.array([limit] + counts)


def ragged(key, count, total, reach, lean):
    if count == 2:
        one = jax.random.randint(key, (), max(1, total - reach), min(reach, total - 1) + 1)
        return jnp.stack([one, total - one])
    sizes = jnp.asarray(length_profile(count, total, reach, lean), jnp.int32)
    twos = (count - 1) // 2
    donor, receiver = sizes[1:1 + 2 * twos:2], sizes[2:2 + 2 * twos:2]
    room = jnp.minimum(donor - 1, reach - receiver)
    moved = jax.random.randint(jax.random.fold_in(key, 1), (twos,), 0, 1 << 20) % (room + 1)
    sizes = sizes.at[1:1 + 2 * twos:2].set(donor - moved).at[2:2 + 2 * twos:2].set(receiver + moved)
    return sizes[jax.random.permutation(jax.random.fold_in(key, 2), count)]


def gaussian(stream_key, extent, width, most, pieces=(), kind=jnp.bfloat16):
    values = width * jax.random.normal(stream_key, extent, jnp.float32)
    if pieces:
        values = values * steps_of(stream_key, extent, pieces, -0.22, 0.18)
    return jnp.clip(values, -most, most).astype(kind)


def setup_inputs(seed: int = 0) -> dict:
    key_of = jax.random.split(jax.random.key(seed), 22)
    inputs = gaussian(key_of[0], (MB, BATCH, SEQ, D), 1.0, 6.0, ((1, 32),))
    cotangent = gaussian(key_of[1], (MB, BATCH, SEQ, D), 1.0, 6.0, ((1, 32),))
    lengths = jax.vmap(lambda own: ragged(own, NDOC, SEQ, SEQ // 2, 2))(jax.random.split(key_of[2], MB * BATCH)).reshape((MB, BATCH, NDOC)).astype(jnp.int32)
    weight_qkv = gaussian(key_of[3], (D, 3 * D), D ** -0.5, 0.1875, ((0, 32),), jnp.float32)
    weight_out = gaussian(key_of[4], (D, D), D ** -0.5, 0.1875, ((0, 32),), jnp.float32)
    weight_up = gaussian(key_of[5], (D, FF), D ** -0.5, 0.1875, ((0, 32),), jnp.float32)
    weight_down = gaussian(key_of[6], (FF, D), FF ** -0.5, 0.09375, ((0, 32),), jnp.float32)
    param_table = draw_param_table(jax.random.fold_in(key_of[21], 71), 0)
    head_scale = jnp.clip(jnp.exp(jax.random.uniform(key_of[8], (HEADS,), jnp.float32, math.log(0.5), math.log(2.0))), 0.5, 2.0)
    moment_qkv = gaussian(key_of[9], (D, 3 * D), (TOKENS ** 0.5), 1024.0, ((0, 32),), jnp.float32)
    square_qkv = jnp.clip(jnp.exp(math.log(262144.0) - 2.7725887 * jax.random.uniform(key_of[10], (D, 3 * D), jnp.float32) ** steps_of(key_of[10], (D, 3 * D), ((0, 32),), -0.2, 0.2)), 16384.0, 262144.0)
    moment_out = gaussian(key_of[11], (D, D), (TOKENS ** 0.5), 1024.0, ((0, 32),), jnp.float32)
    square_out = jnp.clip(jnp.exp(math.log(262144.0) - 2.7725887 * jax.random.uniform(key_of[12], (D, D), jnp.float32) ** steps_of(key_of[12], (D, D), ((0, 32),), -0.2, 0.2)), 16384.0, 262144.0)
    moment_up = gaussian(key_of[13], (D, FF), (TOKENS ** 0.5), 1024.0, ((0, 32),), jnp.float32)
    square_up = jnp.clip(jnp.exp(math.log(262144.0) - 2.7725887 * jax.random.uniform(key_of[14], (D, FF), jnp.float32) ** steps_of(key_of[14], (D, FF), ((0, 32),), -0.2, 0.2)), 16384.0, 262144.0)
    moment_down = gaussian(key_of[15], (FF, D), (TOKENS ** 0.5), 1024.0, ((0, 32),), jnp.float32)
    square_down = jnp.clip(jnp.exp(math.log(262144.0) - 2.7725887 * jax.random.uniform(key_of[16], (FF, D), jnp.float32) ** steps_of(key_of[16], (FF, D), ((0, 32),), -0.2, 0.2)), 16384.0, 262144.0)
    moment_table = gaussian(key_of[17], (VR, D), (TOKENS ** 0.5), 1024.0, ((1, 32),), jnp.float32)
    square_table = jnp.clip(jnp.exp(math.log(262144.0) - 2.7725887 * jax.random.uniform(key_of[18], (VR, D), jnp.float32) ** steps_of(key_of[18], (VR, D), ((1, 32),), -0.2, 0.2)), 16384.0, 262144.0)
    moment_heads = gaussian(key_of[19], (HEADS,), (TOKENS ** 0.5), 1024.0, (), jnp.float32)
    square_heads = jnp.clip(jnp.exp(jax.random.uniform(key_of[20], (HEADS,), jnp.float32, math.log(16384.0), math.log(262144.0))), 16384.0, 262144.0)
    return dict(inputs=inputs, cotangent=cotangent, lengths=lengths, weight_qkv=weight_qkv, weight_out=weight_out, weight_up=weight_up, weight_down=weight_down, param_table=param_table, head_scale=head_scale, moment_qkv=moment_qkv, square_qkv=square_qkv, moment_out=moment_out, square_out=square_out, moment_up=moment_up, square_up=square_up, moment_down=moment_down, square_down=square_down, moment_table=moment_table, square_table=square_table, moment_heads=moment_heads, square_heads=square_heads)


@jax.custom_vjp
def low(v):
    return lax.optimization_barrier(v.astype(jnp.bfloat16)).astype(jnp.float32)

@jax.custom_vjp
def low_back(v):
    return v

def low_keep(v):
    return (low(v), None)

def low_pass(kept, grad):
    return (grad,)

def back_keep(v):
    return (v, None)

def back_low(kept, grad):
    return (low(grad),)
low.defvjp(low_keep, low_pass)
low_back.defvjp(back_keep, back_low)
norm_eps = 1e-05
beta_one = 0.5
beta_two = 0.5
adam_eps = 1e-06
decay_rate = 0.01
rate_matrix = 0.5
rate_vector = 0.3
masked_value = -1e+30
highest = lax.Precision.HIGHEST

def layer_norm(value, gain, shift):
    center = value - lax.optimization_barrier(jnp.mean(value, axis=-1, keepdims=True))
    spread = lax.optimization_barrier(jnp.mean(center * center, axis=-1, keepdims=True))
    return center * lax.rsqrt(spread + norm_eps) * gain + shift

def unpack(table):
    blocks = FF // D
    base = 3 + blocks
    return dict(gain_in=table[0], gain_attn=table[1], gain_mid=table[2], gain_ffn=table[3:base].reshape(FF), shift_in=table[base], bias_query=table[base + 1], bias_value=table[base + 2], bias_out=table[base + 3], shift_attn=table[base + 4], shift_mid=table[base + 5], bias_down=table[base + 6], bias_up=table[base + 7:base + 7 + blocks].reshape(FF), shift_ffn=table[base + 7 + blocks:base + 7 + 2 * blocks].reshape(FF))

def groups(lens):
    ends = jnp.cumsum(lens).astype(jnp.int32)
    places = jnp.arange(SEQ, dtype=jnp.int32)
    member = lax.optimization_barrier(jnp.sum((places[:, None] >= ends[None, :]).astype(jnp.int32), axis=1))
    return (member, places)

def live_rows(lens):
    member, places = groups(lens)
    return (member < lens.shape[0] - 1).astype(jnp.float32)

def visible(lens):
    member, places = groups(lens)
    live = member < lens.shape[0] - 1
    same = (member[:, None] == member[None, :]) & (places[None, :] <= places[:, None])
    return same & (live[:, None] | (places[None, :] == places[:, None]))

def attend_row(pack_in):
    queries, keys_part, values_part, lens = pack_in
    mask = visible(lens)
    scores = low_back(jnp.einsum('qhd,khd->hqk', queries, keys_part, precision=highest) * HD ** (-0.5))
    scores = jnp.where(mask[None], scores, masked_value)
    top = lax.optimization_barrier(jnp.max(scores, axis=-1, keepdims=True))
    expo = jnp.exp(scores - top)
    probs = expo / lax.optimization_barrier(jnp.sum(expo, axis=-1, keepdims=True))
    return jnp.einsum('hqk,khd->qhd', low(probs), values_part, precision=highest)

def layer(rows, lens, weight_qkv, weight_out, weight_up, weight_down, table, heads):
    params = unpack(low(table))
    count = rows.shape[0]
    normed = low(layer_norm(rows, params['gain_in'], params['shift_in']))
    bias_qkv = jnp.concatenate([params['bias_query'], jnp.zeros((D,), jnp.float32), params['bias_value']])
    projected = low(low_back(jnp.einsum('rsd,de->rse', normed, low(weight_qkv), precision=highest) + bias_qkv))
    queries = projected[..., :D].reshape(count, SEQ, HEADS, HD)
    keys_part = projected[..., D:2 * D].reshape(count, SEQ, HEADS, HD)
    values_part = projected[..., 2 * D:].reshape(count, SEQ, HEADS, HD)
    attended = lax.map(jax.checkpoint(attend_row), (queries, keys_part, values_part, lens))
    attended = low_back(attended)
    scaled = low((attended * heads[None, None, :, None]).reshape(count, SEQ, D))
    attn_pre = low_back(jnp.einsum('rse,ed->rsd', scaled, low(weight_out), precision=highest) + params['bias_out'])
    middle = rows + layer_norm(attn_pre, params['gain_attn'], params['shift_attn'])
    normed_mid = low(layer_norm(middle, params['gain_mid'], params['shift_mid']))
    up_pre = low_back(jnp.einsum('rsd,df->rsf', normed_mid, low(weight_up), precision=highest) + params['bias_up'])
    hidden = low(layer_norm(jax.nn.gelu(up_pre), params['gain_ffn'], params['shift_ffn']))
    down = low_back(jnp.einsum('rsf,fd->rsd', hidden, low(weight_down), precision=highest) + params['bias_down'])
    return middle + down

def adam_terms(grad, moment, square):
    fresh_moment = beta_one * moment + (1.0 - beta_one) * grad
    fresh_square = beta_two * square + (1.0 - beta_two) * grad * grad
    direction = fresh_moment / (1.0 - beta_one ** STEP) / (jnp.sqrt(fresh_square / (1.0 - beta_two ** STEP)) + adam_eps)
    return (fresh_moment, fresh_square, direction)

def reference(inputs, cotangent, lengths, weight_qkv, weight_out, weight_up, weight_down, param_table, head_scale, moment_qkv, square_qkv, moment_out, square_out, moment_up, square_up, moment_down, square_down, moment_table, square_table, moment_heads, square_heads):
    params_all = (weight_qkv, weight_out, weight_up, weight_down, param_table, head_scale)

    def one_batch(carry, batch):
        rows, back, lens = batch

        def forward(rows_f, wq, wo, wu, wd, table, heads):
            return layer(rows_f, lens, wq, wo, wu, wd, table, heads)
        result, pull = jax.vjp(forward, rows.astype(jnp.float32), *params_all)
        live = jax.vmap(live_rows)(lens)
        grads = pull(back.astype(jnp.float32) * live[:, :, None])
        fresh = tuple((total + grad for total, grad in zip(carry, grads[1:])))
        return (fresh, (result.astype(jnp.bfloat16), grads[0]))
    start = tuple((jnp.zeros_like(param) for param in params_all))
    totals, (layer_out, input_grad) = lax.scan(one_batch, start, (inputs, cotangent, lengths))
    mats = (weight_qkv, weight_out, weight_up, weight_down)
    moms = (moment_qkv, moment_out, moment_up, moment_down)
    squares = (square_qkv, square_out, square_up, square_down)
    results = []
    stats = []
    for position in range(4):
        fresh_moment, fresh_square, direction = adam_terms(totals[position], moms[position], squares[position])
        update = direction + decay_rate * mats[position]
        weight_norm = jnp.sqrt(jnp.sum(mats[position] * mats[position]))
        update_norm = jnp.sqrt(jnp.sum(update * update))
        ratio = weight_norm / update_norm
        results.append((mats[position] - rate_matrix * ratio * update, fresh_moment, fresh_square))
        stats.append(jnp.stack([weight_norm, update_norm, ratio]))
    table_moment, table_square, table_dir = adam_terms(totals[4], moment_table, square_table)
    heads_moment, heads_square, heads_dir = adam_terms(totals[5], moment_heads, square_heads)
    lamb_stats = jnp.stack(stats)
    return (layer_out, input_grad, results[0][0], results[0][1], results[0][2], results[1][0], results[1][1], results[1][2], results[2][0], results[2][1], results[2][2], results[3][0], results[3][1], results[3][2], param_table - rate_vector * table_dir, table_moment, table_square, head_scale - rate_vector * heads_dir, heads_moment, heads_square, lamb_stats)
```

```python
import functools

import jax
import jax.numpy as jnp
from jax import lax
from jax.sharding import PartitionSpec as P

HEADS = 16
HD = 64
FF = 4096
STEP = 5


norm_eps = 1e-05
beta_one = 0.5
beta_two = 0.5
adam_eps = 1e-06
decay_rate = 0.01
rate_matrix = 0.5
rate_vector = 0.3
masked_value = -1e30
table_order = (
    "gain_in",
    "gain_attn",
    "gain_mid",
    "gain_ffn",
    "shift_in",
    "bias_query",
    "bias_value",
    "bias_out",
    "shift_attn",
    "shift_mid",
    "bias_down",
    "bias_up",
    "shift_ffn",
)


def layer_norm(value, gain, shift):
    center = value - jnp.mean(value, axis=-1, keepdims=True)
    spread = jnp.mean(center * center, axis=-1, keepdims=True)
    return center * lax.rsqrt(spread + norm_eps) * gain + shift


def ffn_norm(value, gain, shift):
    return layer_norm(jax.nn.gelu(value), gain, shift)


def unpack(table):
    width = table.shape[1]
    blocks = FF // width
    base = 3 + blocks
    return dict(
        gain_in=table[0],
        gain_attn=table[1],
        gain_mid=table[2],
        gain_ffn=table[3:base].reshape(FF),
        shift_in=table[base],
        bias_query=table[base + 1],
        bias_value=table[base + 2],
        bias_out=table[base + 3],
        shift_attn=table[base + 4],
        shift_mid=table[base + 5],
        bias_down=table[base + 6],
        bias_up=table[base + 7 : base + 7 + blocks].reshape(FF),
        shift_ffn=table[base + 7 + blocks : base + 7 + 2 * blocks].reshape(FF),
    )


def pack(parts, width):
    return jnp.concatenate([parts[label].reshape(-1, width) for label in table_order], axis=0)


def visible(lens, length):
    ends = jnp.cumsum(lens)
    places = jnp.arange(length, dtype=jnp.int32)
    member = jnp.sum((places[:, None] >= ends[None, :]).astype(jnp.int32), axis=1)
    live = member < lens.shape[0] - 1
    same = (member[:, None] == member[None, :]) & (places[None, :] <= places[:, None])
    mask = same & (live[:, None] | (places[None, :] == places[:, None]))
    return (mask, live.astype(jnp.float32))


def split_heads(projected, width):
    count, length = projected.shape[:2]
    queries = projected[..., :width].reshape(count, length, HEADS, HD)
    keys_part = projected[..., width : 2 * width].reshape(count, length, HEADS, HD)
    values_part = projected[..., 2 * width :].reshape(count, length, HEADS, HD)
    return (queries, keys_part, values_part)


def masked_scores(queries, keys_part, mask):
    scores = jnp.einsum(
        "mqhd,mkhd->mhqk", queries, keys_part, preferred_element_type=jnp.float32
    ) * HD ** (-0.5)
    return jnp.where(mask[:, None], scores, masked_value)


def attend(projected, mask, width):
    queries, keys_part, values_part = split_heads(projected, width)
    scores = masked_scores(queries, keys_part, mask)
    top = jnp.max(scores, axis=-1, keepdims=True)
    expo = jnp.exp(scores - top)
    total = jnp.sum(expo, axis=-1, keepdims=True)
    probs = expo / total
    log_total = top + jnp.log(total)
    attended = jnp.einsum(
        "mhqk,mkhd->mqhd",
        probs.astype(jnp.bfloat16),
        values_part,
        preferred_element_type=jnp.float32,
    )
    return attended, log_total


def attend_back(projected, mask, width, d_att, log_total):
    queries, keys_part, values_part = split_heads(projected, width)
    count, length = projected.shape[:2]
    probs = jnp.exp(masked_scores(queries, keys_part, mask) - log_total)
    grad_values = jnp.einsum(
        "mhqk,mqhd->mkhd", probs.astype(jnp.bfloat16), d_att, preferred_element_type=jnp.float32
    )
    d_probs = jnp.einsum("mqhd,mkhd->mhqk", d_att, values_part, preferred_element_type=jnp.float32)
    inner = jnp.sum(d_probs * probs, axis=-1, keepdims=True)
    d_scores = (probs * (d_probs - inner)).astype(jnp.bfloat16)
    factor = HD ** (-0.5)
    grad_queries = (
        jnp.einsum("mhqk,mkhd->mqhd", d_scores, keys_part, preferred_element_type=jnp.float32)
        * factor
    )
    grad_keys = (
        jnp.einsum("mhqk,mqhd->mkhd", d_scores, queries, preferred_element_type=jnp.float32)
        * factor
    )
    return jnp.concatenate(
        [item.reshape(count, length, width) for item in (grad_queries, grad_keys, grad_values)],
        axis=-1,
    ).astype(jnp.bfloat16)


def weight_grad(left, right):
    return jnp.einsum("sa,sb->ab", left, right, preferred_element_type=jnp.float32).astype(
        jnp.bfloat16
    )


def adam_terms(grad, moment, square):
    fresh_moment = beta_one * moment + (1.0 - beta_one) * grad
    fresh_square = beta_two * square + (1.0 - beta_two) * grad * grad
    direction = (
        fresh_moment
        / (1.0 - beta_one**STEP)
        / (jnp.sqrt(fresh_square / (1.0 - beta_two**STEP)) + adam_eps)
    )
    return (fresh_moment, fresh_square, direction)


AXES = ("dp", "sub")


class Ring:
    def __init__(self, sizes):
        self.count = sizes[0] * sizes[1]
        self.bits = self.count.bit_length() - 1
        self.core = 0
        inner = list(range(1, self.bits))
        self.orders = ([0] + inner, [0] + inner[1:2] + inner[0:1] + inner[2:])

    def swap(self, value, bit):
        pairs = [(i, i ^ (1 << bit)) for i in range(self.count)]
        return lax.ppermute(value, AXES, pairs)

    def side(self, bit):
        return (lax.axis_index(AXES) >> bit) & 1

    def scatter_sum(self, grad, order, wire):
        rows = grad.shape[0] // self.count
        width = grad.shape[1]
        view = grad.reshape([2] * self.bits + [rows, width])
        left = list(range(self.bits - 1, -1, -1))
        for bit in order:
            axis = left.index(bit)
            mine = self.side(bit)
            send = lax.dynamic_index_in_dim(view, 1 - mine, axis, keepdims=False).astype(wire)
            keep = lax.dynamic_index_in_dim(view, mine, axis, keepdims=False)
            view = keep.astype(jnp.float32) + self.swap(send, bit).astype(jnp.float32)
            left.remove(bit)
        return view.reshape(rows, width)

    def gather(self, shard, order):
        rows, width = shard.shape
        have = []
        value = shard.reshape(1, rows, width)
        for bit in reversed(order):
            other = self.swap(value, bit)
            post = 1 << sum(1 for seen in have if seen < bit)
            pre = value.shape[0] // post
            first = self.side(bit) == 0
            own = value.reshape(pre, 1, post, rows, width)
            other = other.reshape(pre, 1, post, rows, width)
            value = jnp.concatenate(
                [jnp.where(first, own, other), jnp.where(first, other, own)], axis=1
            ).reshape(2 * pre * post, rows, width)
            have.append(bit)
        return value.reshape(self.count * rows, width)

    def gather_both(self, shard):
        half = shard.shape[1] // 2
        return jnp.concatenate(
            [
                self.gather(shard[:, :half], self.orders[0]),
                self.gather(shard[:, half:], self.orders[1]),
            ],
            axis=1,
        )

    def scatter_both(self, grad):
        half = grad.shape[1] // 2
        return jnp.concatenate(
            [
                self.scatter_sum(grad[:, :half], self.orders[0], jnp.bfloat16),
                self.scatter_sum(grad[:, half:], self.orders[1], jnp.bfloat16),
            ],
            axis=1,
        )

    def total(self, value):
        for bit in range(self.bits):
            value = value + self.swap(value, bit)
        return value


def per_device(
    ring,
    inputs,
    cotangent,
    lengths,
    weight_qkv,
    weight_out,
    weight_up,
    weight_down,
    param_table,
    head_scale,
    moment_qkv,
    square_qkv,
    moment_out,
    square_out,
    moment_up,
    square_up,
    moment_down,
    square_down,
    moment_table,
    square_table,
    moment_heads,
    square_heads,
):
    count, length, width = inputs.shape[0], inputs.shape[2], inputs.shape[3]
    tokens = count * length
    table_rows = param_table.shape[0]
    piece = param_table.shape[1]
    low = jnp.bfloat16

    table_all = ring.gather(
        param_table.astype(low).reshape(1, table_rows * piece), ring.orders[0]
    ).reshape(ring.count, table_rows, piece)
    params = unpack(table_all.transpose(1, 0, 2).reshape(table_rows, width).astype(jnp.float32))
    w_qkv = ring.gather_both(weight_qkv.astype(low))
    w_qkv, shard_out, shard_up, shard_down = lax.optimization_barrier(
        (w_qkv, weight_out.astype(low), weight_up.astype(low), weight_down.astype(low))
    )
    w_out = ring.gather_both(shard_out)
    w_up = ring.gather_both(shard_up)
    w_down = ring.gather_both(shard_down)

    mask, live = jax.vmap(lambda lens: visible(lens, length))(lengths[:, 0])
    live = live.reshape(tokens, 1)
    row = inputs.reshape(tokens, width).astype(jnp.float32)

    normed = layer_norm(row, params["gain_in"], params["shift_in"]).astype(low)
    bias_qkv = jnp.concatenate(
        [params["bias_query"], jnp.zeros_like(params["bias_query"]), params["bias_value"]]
    )
    projected = (
        (jnp.dot(normed, w_qkv, preferred_element_type=jnp.float32) + bias_qkv)
        .astype(low)
        .reshape(count, length, 3 * width)
    )
    attended, log_total = attend(projected, mask, width)
    heads = head_scale[None, None, :, None]
    scaled = (attended * heads).reshape(tokens, width).astype(low)
    attn_pre = jnp.dot(scaled, w_out, preferred_element_type=jnp.float32) + params["bias_out"]
    middle = row + layer_norm(attn_pre, params["gain_attn"], params["shift_attn"])
    normed_mid = layer_norm(middle, params["gain_mid"], params["shift_mid"]).astype(low)
    up_pre = jnp.dot(normed_mid, w_up, preferred_element_type=jnp.float32) + params["bias_up"]
    hidden = ffn_norm(up_pre, params["gain_ffn"], params["shift_ffn"]).astype(low)

    back_low = cotangent.reshape(tokens, width) * live.astype(low)
    back = back_low.astype(jnp.float32)
    grad_down = weight_grad(hidden, back_low)
    hidden, grad_down = lax.optimization_barrier((hidden, grad_down))
    result = (
        middle + jnp.dot(hidden, w_down, preferred_element_type=jnp.float32) + params["bias_down"]
    ).astype(low)
    sum_down = ring.scatter_both(grad_down)

    d_hidden = jnp.einsum("sd,fd->sf", back_low, w_down, preferred_element_type=jnp.float32)
    unused, pull = jax.vjp(ffn_norm, up_pre, params["gain_ffn"], params["shift_ffn"])
    d_up, gain_ffn_grad, shift_ffn_grad = pull(d_hidden)
    d_up = d_up.astype(low)
    grad_up = weight_grad(normed_mid, d_up)
    d_up, grad_up = lax.optimization_barrier((d_up, grad_up))
    sum_up = ring.scatter_both(grad_up)
    bias_up_grad = jnp.sum(d_up.astype(jnp.float32), axis=0)
    d_normed_mid = jnp.einsum("sf,df->sd", d_up, w_up, preferred_element_type=jnp.float32)
    unused, pull = jax.vjp(layer_norm, middle, params["gain_mid"], params["shift_mid"])
    d_mid_part, gain_mid_grad, shift_mid_grad = pull(d_normed_mid)
    d_middle = back + d_mid_part
    unused, pull = jax.vjp(layer_norm, attn_pre, params["gain_attn"], params["shift_attn"])
    d_attn, gain_attn_grad, shift_attn_grad = pull(d_middle)
    d_attn = d_attn.astype(low)
    grad_out = weight_grad(scaled, d_attn)
    d_attn, grad_out = lax.optimization_barrier((d_attn, grad_out))
    sum_out = ring.scatter_both(grad_out)
    bias_out_grad = jnp.sum(d_attn.astype(jnp.float32), axis=0)
    d_scaled = jnp.einsum("sd,ed->se", d_attn, w_out, preferred_element_type=jnp.float32).reshape(
        count, length, HEADS, HD
    )
    grad_heads = jnp.sum(d_scaled * attended, axis=(0, 1, 3))
    d_att = (d_scaled * heads).astype(low)
    d_qkv = attend_back(projected, mask, width, d_att, log_total).reshape(tokens, 3 * width)
    grad_qkv = weight_grad(normed, d_qkv)
    d_qkv, grad_qkv = lax.optimization_barrier((d_qkv, grad_qkv))
    sum_qkv = ring.scatter_both(grad_qkv)
    column_sums = jnp.sum(d_qkv.astype(jnp.float32), axis=0)
    d_normed = jnp.einsum("se,de->sd", d_qkv, w_qkv, preferred_element_type=jnp.float32)
    unused, pull = jax.vjp(layer_norm, row, params["gain_in"], params["shift_in"])
    d_row_part, gain_in_grad, shift_in_grad = pull(d_normed)
    grad_row = d_middle + d_row_part
    table_grad = pack(
        dict(
            gain_in=gain_in_grad,
            gain_attn=gain_attn_grad,
            gain_mid=gain_mid_grad,
            gain_ffn=gain_ffn_grad,
            shift_in=shift_in_grad,
            bias_query=column_sums[:width],
            bias_value=column_sums[2 * width :],
            bias_out=bias_out_grad,
            shift_attn=shift_attn_grad,
            shift_mid=shift_mid_grad,
            bias_down=jnp.sum(back, axis=0),
            bias_up=bias_up_grad,
            shift_ffn=shift_ffn_grad,
        ),
        width,
    )
    table_sum = ring.scatter_sum(
        table_grad.reshape(table_rows, ring.count, piece)
        .transpose(1, 0, 2)
        .reshape(ring.count, table_rows * piece),
        ring.orders[0],
        jnp.float32,
    ).reshape(table_rows, piece)
    totals = (sum_qkv, sum_out, sum_up, sum_down, table_sum)

    mats = (weight_qkv, weight_out, weight_up, weight_down)
    moms = (moment_qkv, moment_out, moment_up, moment_down)
    squares = (square_qkv, square_out, square_up, square_down)
    fresh_moms = []
    fresh_squares = []
    updates = []
    for position in range(4):
        fresh_moment, fresh_square, direction = adam_terms(
            totals[position], moms[position], squares[position]
        )
        fresh_moms.append(fresh_moment)
        fresh_squares.append(fresh_square)
        updates.append(direction + decay_rate * mats[position])
    weight_sq = jnp.stack([jnp.sum(item * item) for item in mats])
    update_sq = jnp.stack([jnp.sum(item * item) for item in updates])
    sums = ring.total(jnp.concatenate([grad_heads, weight_sq, update_sq]))
    head_sum = sums[:HEADS]
    weight_norm = jnp.sqrt(sums[HEADS : HEADS + 4])
    update_norm = jnp.sqrt(sums[HEADS + 4 :])
    ratio = weight_norm / update_norm
    new_mats = [
        mats[position] - rate_matrix * ratio[position] * updates[position] for position in range(4)
    ]
    table_moment, table_square, table_dir = adam_terms(totals[4], moment_table, square_table)
    heads_moment, heads_square, heads_dir = adam_terms(head_sum, moment_heads, square_heads)
    lamb_stats = jnp.stack([weight_norm, update_norm, ratio], axis=1)
    layer_out = result.reshape(inputs.shape)
    input_grad = grad_row.reshape(inputs.shape)
    return (
        layer_out,
        input_grad,
        new_mats[0],
        fresh_moms[0],
        fresh_squares[0],
        new_mats[1],
        fresh_moms[1],
        fresh_squares[1],
        new_mats[2],
        fresh_moms[2],
        fresh_squares[2],
        new_mats[3],
        fresh_moms[3],
        fresh_squares[3],
        param_table - rate_vector * table_dir,
        table_moment,
        table_square,
        head_scale - rate_vector * heads_dir,
        heads_moment,
        heads_square,
        lamb_stats,
    )


def solution(mesh):
    ring = Ring((mesh.shape["dp"], mesh.shape["sub"]))
    placed = (
        P(None, ("dp", "sub"), None, None),
        P(None, ("dp", "sub"), None, None),
        P(None, ("dp", "sub"), None),
        P(("dp", "sub"), None),
        P(("dp", "sub"), None),
        P(("dp", "sub"), None),
        P(("dp", "sub"), None),
        P(None, ("dp", "sub")),
        P(),
        P(("dp", "sub"), None),
        P(("dp", "sub"), None),
        P(("dp", "sub"), None),
        P(("dp", "sub"), None),
        P(("dp", "sub"), None),
        P(("dp", "sub"), None),
        P(("dp", "sub"), None),
        P(("dp", "sub"), None),
        P(None, ("dp", "sub")),
        P(None, ("dp", "sub")),
        P(),
        P(),
    )
    return jax.shard_map(
        functools.partial(per_device, ring),
        mesh=mesh,
        in_specs=placed,
        out_specs=(
            P(None, ("dp", "sub"), None, None),
            P(None, ("dp", "sub"), None, None),
            P(("dp", "sub"), None),
            P(("dp", "sub"), None),
            P(("dp", "sub"), None),
            P(("dp", "sub"), None),
            P(("dp", "sub"), None),
            P(("dp", "sub"), None),
            P(("dp", "sub"), None),
            P(("dp", "sub"), None),
            P(("dp", "sub"), None),
            P(("dp", "sub"), None),
            P(("dp", "sub"), None),
            P(("dp", "sub"), None),
            P(None, ("dp", "sub")),
            P(None, ("dp", "sub")),
            P(None, ("dp", "sub")),
            P(),
            P(),
            P(),
            P(),
        ),
        check_vma=False,
    )
```

```python
import functools

import jax
import jax.numpy as jnp
from jax import lax
from jax.experimental import pallas as pl
from jax.experimental.pallas import tpu as pltpu
from jax.sharding import PartitionSpec as P

HEADS = 16
HD = 64
FF = 4096
STEP = 5
BLOCK = 256


norm_eps = 1e-05
beta_one = 0.5
beta_two = 0.5
adam_eps = 1e-06
decay_rate = 0.01
rate_matrix = 0.5
rate_vector = 0.3
masked_value = -1e30
table_order = (
    "gain_in",
    "gain_attn",
    "gain_mid",
    "gain_ffn",
    "shift_in",
    "bias_query",
    "bias_value",
    "bias_out",
    "shift_attn",
    "shift_mid",
    "bias_down",
    "bias_up",
    "shift_ffn",
)


def layer_norm(value, gain, shift):
    center = value - jnp.mean(value, axis=-1, keepdims=True)
    spread = jnp.mean(center * center, axis=-1, keepdims=True)
    return center * lax.rsqrt(spread + norm_eps) * gain + shift


def ffn_norm(value, gain, shift):
    return layer_norm(jax.nn.gelu(value), gain, shift)


def unpack(table):
    width = table.shape[1]
    blocks = FF // width
    base = 3 + blocks
    return dict(
        gain_in=table[0],
        gain_attn=table[1],
        gain_mid=table[2],
        gain_ffn=table[3:base].reshape(FF),
        shift_in=table[base],
        bias_query=table[base + 1],
        bias_value=table[base + 2],
        bias_out=table[base + 3],
        shift_attn=table[base + 4],
        shift_mid=table[base + 5],
        bias_down=table[base + 6],
        bias_up=table[base + 7 : base + 7 + blocks].reshape(FF),
        shift_ffn=table[base + 7 + blocks : base + 7 + 2 * blocks].reshape(FF),
    )


def pack(parts, width):
    return jnp.concatenate([parts[label].reshape(-1, width) for label in table_order], axis=0)


def lane_masks(dtype):
    lane = lax.broadcasted_iota(jnp.int32, (1, 2 * HD), 1)
    first = (lane < HD).astype(jnp.float32)
    return first.astype(dtype), (1.0 - first).astype(dtype)


def write_bias(code_col, code_row, bias_ref):
    length = bias_ref.shape[0]
    source = lax.broadcasted_iota(jnp.int32, (length, length), 0)
    target = lax.broadcasted_iota(jnp.int32, (length, length), 1)
    same = (code_col[0] == code_row[0]) & (source <= target)
    bias_ref[...] = jnp.where(same, 0.0, masked_value)


def dot_rows(left, right):
    return lax.dot_general(
        left, right, (((1,), (1,)), ((), ())), preferred_element_type=jnp.float32
    )


def dot_firsts(left, right):
    return lax.dot_general(
        left, right, (((0,), (0,)), ((), ())), preferred_element_type=jnp.float32
    )


def attend_kernel(code_col, code_row, q_ref, k_ref, v_ref, heads, att_ref, out_ref, log_ref, bias):
    @pl.when(pl.program_id(1) == 0)
    def _():
        write_bias(code_col, code_row, bias)

    masks = lane_masks(jnp.bfloat16)
    keep_first = lane_masks(jnp.float32)[0]
    factor = HD ** (-0.5)
    for start in range(0, q_ref.shape[1], BLOCK):
        stop = start + BLOCK
        queries = q_ref[0, start:stop] * jnp.bfloat16(factor)
        keys = k_ref[0, :stop]
        values = v_ref[0, :stop]
        parts = []
        for head in range(2):
            scores = dot_rows(keys, queries * masks[head]) + bias[:stop, start:stop]
            top = jnp.max(scores, axis=0, keepdims=True)
            expo = jnp.exp(scores - top)
            total = jnp.sum(expo, axis=0, keepdims=True)
            probs = (expo * (1.0 / total)).astype(jnp.bfloat16)
            log_ref[0, 0, head : head + 1, start:stop] = top + jnp.log(total)
            parts.append(dot_firsts(probs, values))
        attended = jnp.where(keep_first > 0.5, parts[0], parts[1])
        att_ref[0, start:stop] = attended
        out_ref[0, start:stop] = (attended * heads[...]).astype(jnp.bfloat16)


def attend_back_kernel(
    code_col,
    code_row,
    q_ref,
    k_ref,
    v_ref,
    heads,
    log_ref,
    grad_ref,
    att_ref,
    dq_ref,
    dk_ref,
    dv_ref,
    heads_ref,
    bias,
    sum_k,
    sum_v,
):
    @pl.when(pl.program_id(1) == 0)
    def _():
        write_bias(code_col, code_row, bias)

    masks = lane_masks(jnp.bfloat16)
    factor = HD ** (-0.5)
    heads_ref[0, 0] = jnp.sum(grad_ref[0] * att_ref[0], axis=0, keepdims=True)
    sum_k[...] = jnp.zeros_like(sum_k)
    sum_v[...] = jnp.zeros_like(sum_v)
    for start in range(0, q_ref.shape[1], BLOCK):
        stop = start + BLOCK
        queries = q_ref[0, start:stop] * jnp.bfloat16(factor)
        keys = k_ref[0, :stop]
        values = v_ref[0, :stop]
        d_att = (grad_ref[0, start:stop] * heads[...]).astype(jnp.bfloat16)
        d_queries = None
        for head in range(2):
            own_queries = queries * masks[head]
            own_grads = d_att * masks[head]
            scores = dot_rows(keys, own_queries) + bias[:stop, start:stop]
            probs = jnp.exp(scores - log_ref[0, 0, head : head + 1, start:stop])
            d_probs = dot_rows(values, own_grads)
            inner = jnp.sum(d_probs * probs, axis=0, keepdims=True)
            d_scores = (probs * (d_probs - inner)).astype(jnp.bfloat16)
            sum_v[:stop] += jnp.dot(
                probs.astype(jnp.bfloat16), own_grads, preferred_element_type=jnp.float32
            )
            sum_k[:stop] += jnp.dot(d_scores, own_queries, preferred_element_type=jnp.float32)
            part = dot_firsts(d_scores, keys * masks[head])
            d_queries = part if d_queries is None else d_queries + part
        dq_ref[0, start:stop] = (d_queries * factor).astype(jnp.bfloat16)
    dk_ref[0] = sum_k[...].astype(jnp.bfloat16)
    dv_ref[0] = sum_v[...].astype(jnp.bfloat16)


def attention_specs(length, width):
    pairs = width // (2 * HD)
    column = pl.BlockSpec((1, length, 1), lambda m, j: (m, 0, 0))
    line = pl.BlockSpec((1, 1, length), lambda m, j: (m, 0, 0))
    parts = [
        pl.BlockSpec((1, length, 2 * HD), lambda m, j, part=part: (m, 0, j + part * pairs))
        for part in range(3)
    ]
    scale = pl.BlockSpec((1, 2 * HD), lambda m, j: (0, j))
    logs = pl.BlockSpec((1, 1, 2, length), lambda m, j: (m, j, 0, 0))
    tile = pl.BlockSpec((1, length, 2 * HD), lambda m, j: (m, 0, j))
    sums = pl.BlockSpec((1, 1, 1, 2 * HD), lambda m, j: (m, j, 0, 0))
    return pairs, column, line, parts, scale, logs, tile, sums


def attend(projected, codes, heads):
    count, length, width = projected.shape[0], projected.shape[1], projected.shape[2] // 3
    pairs, column, line, parts, scale, logs, tile, sums = attention_specs(length, width)
    area = count * HEADS * length * length
    return pl.pallas_call(
        attend_kernel,
        grid=(count, pairs),
        in_specs=[column, line, *parts, scale],
        out_specs=[tile, tile, logs],
        out_shape=[
            jax.ShapeDtypeStruct((count, length, width), jnp.float32),
            jax.ShapeDtypeStruct((count, length, width), jnp.bfloat16),
            jax.ShapeDtypeStruct((count, pairs, 2, length), jnp.float32),
        ],
        scratch_shapes=[pltpu.VMEM((length, length), jnp.float32)],
        cost_estimate=pl.CostEstimate(
            flops=16 * HD * area, transcendentals=area, bytes_accessed=24 * count * length * width
        ),
        name="attend",
    )(codes[:, :, None], codes[:, None, :], projected, projected, projected, heads)


def attend_back(projected, codes, heads, log_total, d_scaled, attended):
    count, length, width = projected.shape[0], projected.shape[1], projected.shape[2] // 3
    pairs, column, line, parts, scale, logs, tile, sums = attention_specs(length, width)
    area = count * HEADS * length * length
    piece = jax.ShapeDtypeStruct((count, length, width), jnp.bfloat16)
    dq, dk, dv, head_sums = pl.pallas_call(
        attend_back_kernel,
        grid=(count, pairs),
        in_specs=[column, line, *parts, scale, logs, tile, tile],
        out_specs=[tile, tile, tile, sums],
        out_shape=[
            piece,
            piece,
            piece,
            jax.ShapeDtypeStruct((count, pairs, 1, 2 * HD), jnp.float32),
        ],
        scratch_shapes=[
            pltpu.VMEM((length, length), jnp.float32),
            pltpu.VMEM((length, 2 * HD), jnp.float32),
            pltpu.VMEM((length, 2 * HD), jnp.float32),
        ],
        cost_estimate=pl.CostEstimate(
            flops=40 * HD * area, transcendentals=area, bytes_accessed=30 * count * length * width
        ),
        name="attend_back",
    )(
        codes[:, :, None],
        codes[:, None, :],
        projected,
        projected,
        projected,
        heads,
        log_total,
        d_scaled,
        attended,
    )
    grad_heads = jnp.sum(head_sums.reshape(count, HEADS, HD), axis=(0, 2))
    return jnp.concatenate([dq, dk, dv], axis=-1), grad_heads


def group_codes(lens, length):
    ends = jnp.cumsum(lens)
    places = jnp.arange(length, dtype=jnp.int32)
    member = jnp.sum((places[:, None] >= ends[None, :]).astype(jnp.int32), axis=1)
    live = member < lens.shape[0] - 1
    return jnp.where(live, member, lens.shape[0] + places), live


def weight_grad(left, right):
    return jnp.einsum("sa,sb->ab", left, right, preferred_element_type=jnp.float32).astype(
        jnp.bfloat16
    )


def adam_terms(grad, moment, square):
    fresh_moment = beta_one * moment + (1.0 - beta_one) * grad
    fresh_square = beta_two * square + (1.0 - beta_two) * grad * grad
    direction = (
        fresh_moment
        / (1.0 - beta_one**STEP)
        / (jnp.sqrt(fresh_square / (1.0 - beta_two**STEP)) + adam_eps)
    )
    return (fresh_moment, fresh_square, direction)


AXES = ("dp", "sub")


class Ring:
    def __init__(self, sizes):
        self.count = sizes[0] * sizes[1]
        self.bits = self.count.bit_length() - 1
        inner = list(range(1, self.bits))
        self.orders = ([0] + inner, [0] + inner[1:2] + inner[0:1] + inner[2:])

    def swap(self, value, bit):
        pairs = [(i, i ^ (1 << bit)) for i in range(self.count)]
        return lax.ppermute(value, AXES, pairs)

    def side(self, bit):
        return (lax.axis_index(AXES) >> bit) & 1

    def total(self, value):
        for bit in range(self.bits):
            value = value + self.swap(value, bit)
        return value


class Gather:
    def __init__(self, ring, shard, order):
        self.ring = ring
        self.rows, self.width = shard.shape
        self.value = shard.reshape(1, self.rows, self.width)
        self.todo = list(reversed(order))
        self.have = []
        self.flight = None

    def land(self):
        if self.flight is None:
            return
        bit = self.have[-1]
        post = 1 << sum(1 for seen in self.have if seen < bit)
        pre = self.value.shape[0] // post
        first = self.ring.side(bit) == 0
        own = self.value.reshape(pre, 1, post, self.rows, self.width)
        other = self.flight.reshape(pre, 1, post, self.rows, self.width)
        self.value = jnp.concatenate(
            [jnp.where(first, own, other), jnp.where(first, other, own)], axis=1
        ).reshape(2 * pre * post, self.rows, self.width)
        self.flight = None

    def step(self):
        self.land()
        bit = self.todo.pop(0)
        self.have.append(bit)
        self.flight = self.ring.swap(self.value, bit)

    def result(self):
        while self.todo:
            self.step()
        self.land()
        return self.value


class Scatter:
    def __init__(self, ring, grad, order, wire=jnp.bfloat16):
        self.ring = ring
        self.rows = grad.shape[0] // ring.count
        self.width = grad.shape[1]
        self.view = grad.reshape([2] * ring.bits + [self.rows, self.width])
        self.left = list(range(ring.bits - 1, -1, -1))
        self.todo = list(order)
        self.wire = wire
        self.flight = None

    def land(self):
        if self.flight is not None:
            self.view = self.view.astype(jnp.float32) + self.flight.astype(jnp.float32)
            self.flight = None

    def step(self):
        self.land()
        bit = self.todo.pop(0)
        axis = self.left.index(bit)
        self.left.remove(bit)
        mine = self.ring.side(bit)
        send = lax.dynamic_index_in_dim(self.view, 1 - mine, axis, keepdims=False)
        self.view = lax.dynamic_index_in_dim(self.view, mine, axis, keepdims=False)
        self.flight = self.ring.swap(send.astype(self.wire), bit)

    def result(self):
        while self.todo:
            self.step()
        self.land()
        return self.view.reshape(self.rows, self.width)


def pair_of(kind, ring, halves):
    return [kind(ring, half, order) for half, order in zip(halves, ring.orders)]


def meet(values, movers):
    values, flights = lax.optimization_barrier(
        (tuple(values), tuple(mover.flight for mover in movers))
    )
    for mover, flight in zip(movers, flights):
        mover.flight = flight
    return values


def step_all(movers):
    for mover in movers:
        mover.step()


def per_device(
    ring,
    inputs,
    cotangent,
    lengths,
    weight_qkv,
    weight_out,
    weight_up,
    weight_down,
    param_table,
    head_scale,
    moment_qkv,
    square_qkv,
    moment_out,
    square_out,
    moment_up,
    square_up,
    moment_down,
    square_down,
    moment_table,
    square_table,
    moment_heads,
    square_heads,
):
    count, length, width = inputs.shape[0], inputs.shape[2], inputs.shape[3]
    tokens = count * length
    table_rows = param_table.shape[0]
    piece = param_table.shape[1]
    low = jnp.bfloat16

    half_qkv = weight_qkv.shape[1] // 2
    low_qkv = weight_qkv.astype(low)
    low_table = jnp.pad(param_table.T.astype(low), ((0, 0), (0, 128 - table_rows)))
    w_out = lax.all_gather(weight_out.astype(low), AXES, axis=0, tiled=True)
    w_up = lax.all_gather(weight_up.astype(low), AXES, axis=0, tiled=True)
    w_down = lax.all_gather(weight_down.astype(low), AXES, axis=0, tiled=True)
    first = pair_of(
        Gather,
        ring,
        (
            low_qkv[:, :half_qkv],
            jnp.concatenate([low_qkv[:, half_qkv:], low_table], axis=1),
        ),
    )
    left = first[0].result().reshape(-1, half_qkv)
    right = first[1].result().reshape(-1, half_qkv + 128)
    w_qkv = jnp.concatenate([left, right[:, :half_qkv]], axis=1)
    table = right[:, half_qkv : half_qkv + table_rows].T.astype(jnp.float32)
    params = unpack(table)

    codes, live = jax.vmap(lambda lens: group_codes(lens, length))(lengths[:, 0])
    live = live.astype(low).reshape(tokens, 1)
    row = inputs.reshape(tokens, width).astype(jnp.float32)
    heads = jnp.repeat(head_scale, HD)[None]

    normed = layer_norm(row, params["gain_in"], params["shift_in"]).astype(low)
    bias_qkv = jnp.concatenate(
        [params["bias_query"], jnp.zeros_like(params["bias_query"]), params["bias_value"]]
    )
    projected = (jnp.dot(normed, w_qkv, preferred_element_type=jnp.float32) + bias_qkv).astype(low)
    projected = projected.reshape(count, length, 3 * width)
    attended, scaled, log_total = attend(projected, codes, heads)
    scaled = scaled.reshape(tokens, width)
    attn_pre = jnp.dot(scaled, w_out, preferred_element_type=jnp.float32) + params["bias_out"]
    middle = row + layer_norm(attn_pre, params["gain_attn"], params["shift_attn"])
    normed_mid = layer_norm(middle, params["gain_mid"], params["shift_mid"]).astype(low)
    up_pre = jnp.dot(normed_mid, w_up, preferred_element_type=jnp.float32) + params["bias_up"]
    hidden = ffn_norm(up_pre, params["gain_ffn"], params["shift_ffn"]).astype(low)
    back_low = cotangent.reshape(tokens, width) * live
    back = back_low.astype(jnp.float32)
    grad_down = weight_grad(hidden, back_low)
    hidden, grad_down = meet((hidden, grad_down), [])
    sum_down = lax.psum_scatter(grad_down, AXES, scatter_dimension=0, tiled=True).astype(jnp.float32)
    result = (
        middle + jnp.dot(hidden, w_down, preferred_element_type=jnp.float32) + params["bias_down"]
    ).astype(low)
    d_hidden = jnp.einsum("sd,fd->sf", back_low, w_down, preferred_element_type=jnp.float32)
    unused, pull = jax.vjp(ffn_norm, up_pre, params["gain_ffn"], params["shift_ffn"])
    d_up, gain_ffn_grad, shift_ffn_grad = pull(d_hidden)
    d_up = d_up.astype(low)
    grad_up = weight_grad(normed_mid, d_up)
    d_up, grad_up = meet((d_up, grad_up), [])
    half = grad_up.shape[1] // 2
    later = pair_of(Scatter, ring, (grad_up[:, :half], grad_up[:, half:]))
    step_all(later)
    bias_up_grad = jnp.sum(d_up.astype(jnp.float32), axis=0)
    d_normed_mid = jnp.einsum("sf,df->sd", d_up, w_up, preferred_element_type=jnp.float32)
    unused, pull = jax.vjp(layer_norm, middle, params["gain_mid"], params["shift_mid"])
    d_mid_part, gain_mid_grad, shift_mid_grad = pull(d_normed_mid)
    d_middle = back + d_mid_part
    (d_middle,) = meet((d_middle,), later)
    step_all(later)
    unused, pull = jax.vjp(layer_norm, attn_pre, params["gain_attn"], params["shift_attn"])
    d_attn, gain_attn_grad, shift_attn_grad = pull(d_middle)
    d_attn = d_attn.astype(low)
    grad_out = weight_grad(scaled, d_attn)
    bias_out_grad = jnp.sum(d_attn.astype(jnp.float32), axis=0)
    d_scaled = jnp.einsum("sd,ed->se", d_attn, w_out, preferred_element_type=jnp.float32)
    grad_out, d_scaled = meet((grad_out, d_scaled), later)
    step_all(later)
    d_qkv, grad_heads = attend_back(
        projected, codes, heads, log_total, d_scaled.reshape(count, length, width), attended
    )
    d_qkv = d_qkv.reshape(tokens, 3 * width)
    (d_qkv,) = meet((d_qkv,), later)
    step_all(later)
    grad_qkv = weight_grad(normed, d_qkv)
    d_qkv, grad_qkv = meet((d_qkv, grad_qkv), later)
    half_last = (grad_qkv.shape[1] + width) // 2
    last = pair_of(
        Scatter,
        ring,
        (
            grad_qkv[:, :half_last],
            jnp.concatenate([grad_qkv[:, half_last:], grad_out], axis=1),
        ),
    )
    step_all(last + later)
    d_normed = jnp.einsum("se,de->sd", d_qkv, w_qkv, preferred_element_type=jnp.float32)
    (d_normed,) = meet((d_normed,), last + later)
    sum_up = jnp.concatenate([item.result() for item in later], axis=1)
    step_all(last)
    column_sums = jnp.sum(d_qkv.astype(jnp.float32), axis=0)
    unused, pull = jax.vjp(layer_norm, row, params["gain_in"], params["shift_in"])
    d_row_part, gain_in_grad, shift_in_grad = pull(d_normed)
    grad_row = d_middle + d_row_part
    table_grad = pack(
        dict(
            gain_in=gain_in_grad,
            gain_attn=gain_attn_grad,
            gain_mid=gain_mid_grad,
            gain_ffn=gain_ffn_grad,
            shift_in=shift_in_grad,
            bias_query=column_sums[:width],
            bias_value=column_sums[2 * width :],
            bias_out=bias_out_grad,
            shift_attn=shift_attn_grad,
            shift_mid=shift_mid_grad,
            bias_down=jnp.sum(back, axis=0),
            bias_up=bias_up_grad,
            shift_ffn=shift_ffn_grad,
        ),
        width,
    )
    spread = Scatter(
        ring,
        table_grad.reshape(table_rows, ring.count, piece)
        .transpose(1, 0, 2)
        .reshape(ring.count, table_rows * piece),
        ring.orders[0],
        jnp.float32,
    )
    while last[0].todo:
        step_all([spread])
        meet((), last + [spread])
        step_all(last)
    table_sum = spread.result().reshape(table_rows, piece)
    left = last[0].result()
    right = last[1].result()
    sum_qkv = jnp.concatenate([left, right[:, : half_last - width]], axis=1)
    sum_out = right[:, half_last - width :]
    totals = (sum_qkv, sum_out, sum_up, sum_down, table_sum)

    mats = (weight_qkv, weight_out, weight_up, weight_down)
    moms = (moment_qkv, moment_out, moment_up, moment_down)
    squares = (square_qkv, square_out, square_up, square_down)
    fresh_moms = []
    fresh_squares = []
    updates = []
    for position in range(4):
        fresh_moment, fresh_square, direction = adam_terms(
            totals[position], moms[position], squares[position]
        )
        fresh_moms.append(fresh_moment)
        fresh_squares.append(fresh_square)
        updates.append(direction + decay_rate * mats[position])
    weight_sq = jnp.stack([jnp.sum(item * item) for item in mats])
    update_sq = jnp.stack([jnp.sum(item * item) for item in updates])
    sums = ring.total(jnp.concatenate([grad_heads, weight_sq, update_sq]))
    head_sum = sums[:HEADS]
    weight_norm = jnp.sqrt(sums[HEADS : HEADS + 4])
    update_norm = jnp.sqrt(sums[HEADS + 4 :])
    ratio = weight_norm / update_norm
    new_mats = [
        mats[position] - rate_matrix * ratio[position] * updates[position] for position in range(4)
    ]
    table_moment, table_square, table_dir = adam_terms(totals[4], moment_table, square_table)
    heads_moment, heads_square, heads_dir = adam_terms(head_sum, moment_heads, square_heads)
    lamb_stats = jnp.stack([weight_norm, update_norm, ratio], axis=1)
    layer_out = result.reshape(inputs.shape)
    input_grad = grad_row.reshape(inputs.shape)
    return (
        layer_out,
        input_grad,
        new_mats[0],
        fresh_moms[0],
        fresh_squares[0],
        new_mats[1],
        fresh_moms[1],
        fresh_squares[1],
        new_mats[2],
        fresh_moms[2],
        fresh_squares[2],
        new_mats[3],
        fresh_moms[3],
        fresh_squares[3],
        param_table - rate_vector * table_dir,
        table_moment,
        table_square,
        head_scale - rate_vector * heads_dir,
        heads_moment,
        heads_square,
        lamb_stats,
    )


def solution(mesh):
    ring = Ring((mesh.shape["dp"], mesh.shape["sub"]))
    placed = (
        P(None, ("dp", "sub"), None, None),
        P(None, ("dp", "sub"), None, None),
        P(None, ("dp", "sub"), None),
        P(("dp", "sub"), None),
        P(("dp", "sub"), None),
        P(("dp", "sub"), None),
        P(("dp", "sub"), None),
        P(None, ("dp", "sub")),
        P(),
        P(("dp", "sub"), None),
        P(("dp", "sub"), None),
        P(("dp", "sub"), None),
        P(("dp", "sub"), None),
        P(("dp", "sub"), None),
        P(("dp", "sub"), None),
        P(("dp", "sub"), None),
        P(("dp", "sub"), None),
        P(None, ("dp", "sub")),
        P(None, ("dp", "sub")),
        P(),
        P(),
    )
    return jax.shard_map(
        functools.partial(per_device, ring),
        mesh=mesh,
        in_specs=placed,
        out_specs=(
            P(None, ("dp", "sub"), None, None),
            P(None, ("dp", "sub"), None, None),
            P(("dp", "sub"), None),
            P(("dp", "sub"), None),
            P(("dp", "sub"), None),
            P(("dp", "sub"), None),
            P(("dp", "sub"), None),
            P(("dp", "sub"), None),
            P(("dp", "sub"), None),
            P(("dp", "sub"), None),
            P(("dp", "sub"), None),
            P(("dp", "sub"), None),
            P(("dp", "sub"), None),
            P(("dp", "sub"), None),
            P(None, ("dp", "sub")),
            P(None, ("dp", "sub")),
            P(None, ("dp", "sub")),
            P(),
            P(),
            P(),
            P(),
        ),
        check_vma=False,
    )
```
